512 devices in a mesh: beh: 4 (over y), node: 128 (over x, z, core).
Axes of the slice: x: 4, y: 4, z: 16, core: 2. Of those that a mesh axis runs over, the one named last changes fastest.
Arguments:
- embeddings: bfloat16 [262144, 128], P('node'), may hold values from -16 to 16, as said below
- adjacency: bfloat16 [4, 14336, 128, 128], P('beh', 'node'), may hold values from -0.1875 to 0.1875
- tile_rows: int32 [4, 14336], P('beh', 'node'), may hold values from 0 to 15
- tile_cols: int32 [4, 14336], P('beh', 'node'), may hold values from 0 to 63
- tile_count: int32 [4, 128], P('beh', 'node'), may hold values from 28 to 112, as said below
- need_ids: int32 [4, 8192], P('beh', 'node'), may hold values from 0 to 2047, as said below
- w_query: bfloat16 [128, 128], replicated, may hold values from -0.5 to 0.5
- w_key: bfloat16 [128, 128], replicated, may hold values from -0.5 to 0.5
- w_value: bfloat16 [128, 128], replicated, may hold values from -0.5 to 0.5
- w_out: bfloat16 [128, 128], replicated, may hold values from -0.5 to 0.5
- mlp_gain: float32 [128], replicated, may hold values from 0.1 to 1.9
- w_up: bfloat16 [128, 512], replicated, may hold values from -0.5 to 0.5
- w_down: bfloat16 [512, 128], replicated, may hold values from -0.25 to 0.25
Outputs:
- merged: bfloat16 [4, 262144, 128], P('beh', 'node')
The draws below stay inside these ranges and needn't reach their ends.
Inputs may be any that keep to these rules, and one draw needn't show every extreme that they name: `tile_count`: live slots of one behavior and shard; every behavior has a shard with all 112 slots live. `need_ids`: for each behavior b and shard n, entry n * 64 + m (m < 64) names a block owned by shard 2 m or shard 2 m + 1, block g being owned by shard g // 16. `embeddings`: entries keep within the stated bound.
All inputs are finite; a program needn't handle non-finite values.
Results may differ from the reference program's by a relative error of at most 0.0077.
Values may be sent and summed in bfloat16 or wider, within the bound.
A program may use at most 64 MiB of HBM per device.

```python
import math
import jax
import jax.numpy as jnp
from jax import lax

D = 128
TB = 128
HEADS = 4
HEAD = 32
FF = 512
NODE_DEV = 2048
TILE_DEV = 112
BLK_DEV = 16
NEED = 64
NODES = 262144
N_BEH = 4
N_NODE = 128


def draw_embeddings(key, part):
    base_key = jax.random.fold_in(key, 11)
    entries = jax.random.normal(base_key, (NODES, D), jnp.float32)
    return jnp.clip(entries, -6.0, 6.0).astype(jnp.bfloat16)


def draw_tile_count(key, part):
    counts = jax.random.randint(jax.random.fold_in(key, 21), (N_BEH, N_NODE), TILE_DEV // 4, TILE_DEV + 1)
    where_full = jax.random.randint(jax.random.fold_in(key, 22), (N_BEH,), 0, N_NODE)
    columns = jnp.arange(N_NODE, dtype=jnp.int32)[None, :]
    return jnp.where(columns == where_full[:, None], TILE_DEV, counts).astype(jnp.int32)


def draw_need_ids(key, part):
    parity = jax.random.randint(jax.random.fold_in(key, 31), (N_BEH, N_NODE, NEED), 0, 2)
    owners = 2 * jnp.arange(NEED, dtype=jnp.int32)[None, None, :] + parity
    within = jax.random.randint(jax.random.fold_in(key, 32), (N_BEH, N_NODE, NEED), 0, BLK_DEV)
    return (owners * BLK_DEV + within).reshape(N_BEH, N_NODE * NEED).astype(jnp.int32)


def plant(values, stream_key, least, top_value):
    longest = values.shape.index(max(values.shape))
    spots = []
    for shift in (0, 1):
        where = [jax.random.randint(jax.random.fold_in(stream_key, axis), (), 0, length) for axis, length in enumerate(values.shape)]
        where[longest] = (where[longest] + shift) % values.shape[longest]
        spots.append(tuple(where))
    return values.at[spots[0]].set(least).at[spots[1]].set(top_value)


def levels(stream_key, shape, cuts, smallest, top_value):
    factor_of = 1.0
    for axis_at, blocks in cuts:
        heights = jax.random.uniform(jax.random.fold_in(jax.random.fold_in(stream_key, 6), axis_at), (blocks,), jnp.float32, smallest / len(cuts), top_value / len(cuts))
        factor_of = factor_of * jnp.repeat(jnp.exp(heights), shape[axis_at] // blocks).reshape((-1,) + (1,) * (len(shape) - 1 - axis_at))
    return factor_of


def gaussian(stream_key, shape, deviation, limit, cuts=(), held_as=jnp.bfloat16):
    values = deviation * jax.random.normal(stream_key, shape, jnp.float32)
    if cuts:
        values = values * levels(stream_key, shape, cuts, -0.22, 0.18)
    return jnp.clip(values, -limit, limit).astype(held_as)


def setup_inputs(seed: int = 0) -> dict:
    key_of = jax.random.split(jax.random.key(seed), 14)
    return {
        "embeddings": draw_embeddings(jax.random.fold_in(key_of[13], 71), 0),
        "adjacency": gaussian(key_of[1], (N_BEH, N_NODE * TILE_DEV, TB, TB), (TB * TILE_DEV // BLK_DEV) ** -0.5, 0.1875, ((0, 4), (1, 128))),
        "tile_rows": plant(jax.random.randint(key_of[2], (N_BEH, N_NODE * TILE_DEV), 0, BLK_DEV), jax.random.fold_in(key_of[2], 1), 0, BLK_DEV - 1).astype(jnp.int32),
        "tile_cols": plant(jax.random.randint(key_of[3], (N_BEH, N_NODE * TILE_DEV), 0, NEED), jax.random.fold_in(key_of[3], 1), 0, NEED - 1).astype(jnp.int32),
        "tile_count": draw_tile_count(jax.random.fold_in(key_of[13], 71), 0),
        "need_ids": draw_need_ids(jax.random.fold_in(key_of[13], 71), 0),
        "w_query": gaussian(key_of[6], (D, D), D ** -0.5, 0.5),
        "w_key": gaussian(key_of[7], (D, D), D ** -0.5, 0.5),
        "w_value": gaussian(key_of[8], (D, D), D ** -0.5, 0.5),
        "w_out": gaussian(key_of[9], (D, D), D ** -0.5, 0.5),
        "mlp_gain": jnp.clip(1.0 + 0.18 * jax.random.normal(key_of[10], (D,), jnp.float32), 0.1, 1.9),
        "w_up": gaussian(key_of[11], (D, FF), D ** -0.5, 0.5),
        "w_down": gaussian(key_of[12], (FF, D), FF ** -0.5, 0.25),
    }


def merge_behaviors(behaviors, queries, w_query, w_key, w_value, w_out, mlp_gain, w_up, w_down):
    count_k, row_count, feature = behaviors.shape
    count_q = queries.shape[0]
    flat_keys = behaviors.reshape(count_k * row_count, feature)
    key_rows = jnp.dot(flat_keys, w_key, preferred_element_type=jnp.float32).reshape(count_k, row_count, HEADS, HEAD)
    value_rows = jnp.dot(flat_keys, w_value, preferred_element_type=jnp.float32).reshape(count_k, row_count, HEADS, HEAD)
    flat_queries = queries.reshape(count_q * row_count, feature)
    query_rows = jnp.dot(flat_queries, w_query, preferred_element_type=jnp.float32).reshape(count_q, row_count, HEADS, HEAD)
    scores = jnp.einsum('qrhe,krhe->qrhk', query_rows, key_rows, precision=lax.Precision.HIGHEST) / math.sqrt(HEAD)
    highest = lax.optimization_barrier(jnp.max(scores, axis=-1, keepdims=True))
    weights = jnp.exp(scores - highest)
    weights = weights / lax.optimization_barrier(jnp.sum(weights, axis=-1, keepdims=True))
    mixture = jnp.einsum('qrhk,krhe->qrhe', weights, value_rows, precision=lax.Precision.HIGHEST)
    mixture = mixture.reshape(count_q * row_count, feature).astype(jnp.bfloat16)
    residual = flat_queries.astype(jnp.float32) + jnp.dot(mixture, w_out, preferred_element_type=jnp.float32)
    meansq = lax.optimization_barrier(jnp.mean(residual * residual, axis=-1, keepdims=True))
    normed = (residual * lax.rsqrt(meansq + 1e-06) * mlp_gain.astype(jnp.float32)).astype(jnp.bfloat16)
    hidden = jax.nn.silu(jnp.dot(normed, w_up, preferred_element_type=jnp.float32)).astype(jnp.bfloat16)
    result = residual + jnp.dot(hidden, w_down, preferred_element_type=jnp.float32)
    return result.astype(jnp.bfloat16).reshape(count_q, row_count, feature)

def reference(embeddings, adjacency, tile_rows, tile_cols, tile_count, need_ids, w_query, w_key, w_value, w_out, mlp_gain, w_up, w_down):
    block_total = NODES // TB
    blocks = embeddings.reshape(block_total, TB, D)
    shards = N_BEH * N_NODE
    flat_tiles = adjacency.reshape(shards, TILE_DEV, TB, TB)
    flat_rows = tile_rows.reshape(shards, TILE_DEV)
    flat_cols = tile_cols.reshape(shards, TILE_DEV)
    flat_count = tile_count.reshape(shards)
    flat_need = need_ids.reshape(shards, NEED)
    shard_ids = jnp.arange(shards, dtype=jnp.int32) % N_NODE

    def propagate(pieces):
        tile_block, row_block, col_index, count_now, needed, shard_id = pieces
        sources = blocks[needed[col_index]].astype(jnp.float32)
        product = jnp.einsum('tij,tjd->tid', tile_block.astype(jnp.float32), sources, precision=lax.Precision.HIGHEST)
        active = jnp.arange(TILE_DEV, dtype=jnp.int32) < count_now
        select = ((row_block[:, None] == jnp.arange(BLK_DEV, dtype=jnp.int32)[None, :]) & active[:, None]).astype(jnp.float32)
        summed = jnp.einsum('tb,tid->bid', select, product, precision=lax.Precision.HIGHEST).reshape(NODE_DEV, D)
        start = (shard_id * NODE_DEV).astype(jnp.int32)
        own_rows = lax.dynamic_slice_in_dim(embeddings, start, NODE_DEV, 0)
        return (summed + own_rows.astype(jnp.float32)).astype(jnp.bfloat16)
    spread = lax.map(propagate, (flat_tiles, flat_rows, flat_cols, flat_count, flat_need, shard_ids))
    spread = spread.reshape(N_BEH, N_NODE, NODE_DEV, D)

    def merge_shard(group_rows):
        return merge_behaviors(group_rows, group_rows, w_query, w_key, w_value, w_out, mlp_gain, w_up, w_down)
    merged_all = lax.map(merge_shard, jnp.transpose(spread, (1, 0, 2, 3)))
    return jnp.transpose(merged_all, (1, 0, 2, 3)).reshape(N_BEH, NODES, D)
```

```python
import functools
import math

import jax
import jax.numpy as jnp
from jax import lax
from jax.experimental import pallas as pl
from jax.experimental.pallas import tpu as pltpu
from jax.sharding import PartitionSpec as P

TB = 128
HEADS = 4
HEAD = 32
MESH = pl.DeviceIdType.MESH
STEPS = 8


def place():
    y = lax.axis_index("beh")
    n = lax.axis_index("node")
    return n // 32, y, lax.rem(n // 2, 16), lax.rem(n, 2)


def device(x, y, z, k):
    return (y, (x * 16 + z) * 2 + k)


def gather_kernel(emb_ref, need_ref, out_ref, *scratch):
    chunks = scratch[:9]
    picked, need_v, need_s = scratch[9:12]
    own_sem, pair_send, pair_recv, ring_send, ring_recv = scratch[12:17]
    ask_send, ask_recv, smem_sem, xy_send, xy_recv = scratch[17:]
    x, y, z, k = place()
    me = x * 8 + y * 2 + k
    part = y * 2 + k
    above = device(x, y, lax.rem(z + 1, 16), k)
    below = device(x, y, lax.rem(z + 15, 16), k)
    twin = device(x, y, z, 1 - k)

    def reader(r):
        return device(r // 8, lax.rem(r, 8) // 2, z, lax.rem(r, 2))

    own = pltpu.make_async_copy(
        emb_ref.at[:, part], chunks[0].at[pl.ds(k * 16, 16)], own_sem
    )
    own.start()

    barrier = pltpu.get_barrier_semaphore()

    @pl.loop(1, 32)
    def _(i):
        pl.semaphore_signal(
            barrier, inc=1, device_id=reader(lax.rem(me + i, 32)), device_id_type=MESH
        )

    for neighbour in (above, below):
        pl.semaphore_signal(barrier, inc=1, device_id=neighbour, device_id_type=MESH)
    pl.semaphore_wait(barrier, 33)

    pair = pltpu.make_async_remote_copy(
        src_ref=emb_ref.at[:, y * 2 + 1 - k],
        dst_ref=chunks[0].at[pl.ds(k * 16, 16)],
        send_sem=pair_send,
        recv_sem=pair_recv,
        device_id=twin,
        device_id_type=MESH,
    )
    pair.start()

    @pl.loop(1, 32)
    def _(i):
        pltpu.make_async_remote_copy(
            src_ref=need_ref,
            dst_ref=need_v.at[me],
            send_sem=ask_send,
            recv_sem=ask_recv,
            device_id=reader(lax.rem(me + i, 32)),
            device_id_type=MESH,
        ).start()

    pltpu.make_async_copy(need_ref, need_v.at[me], ask_recv).start()

    def half(step, way, h):
        if step == 0 or step == STEPS:
            return chunks[step].at[pl.ds(h * 16, 16)]
        return chunks[step].at[way, pl.ds(h * 16, 16)]

    def hop(step, way, h):
        return pltpu.make_async_remote_copy(
            src_ref=half(step, way, h),
            dst_ref=half(step + 1, way, h),
            send_sem=ring_send.at[way, step, h],
            recv_sem=ring_recv.at[way, step, h],
            device_id=above if way == 0 else below,
            device_id_type=MESH,
        )

    hops = {}

    def forward(step):
        for h in range(2):
            for way in range(2):
                if step > 0:
                    hops[(step - 1, way, h)].wait_recv()
                if step < STEPS - 1 or way == h:
                    hops[(step, way, h)] = hop(step, way, h)
                    hops[(step, way, h)].start()

    def pick(step):
        @pl.loop(0, 32)
        def _(r):
            if step == 0:
                index = lax.rem(need_s[r, 0, x * 16 + z], 32)
                picked[r, 0] = chunks[0][index]
            elif step == STEPS:
                index = lax.rem(need_s[r, 0, x * 16 + lax.rem(z + 8, 16)], 32)
                picked[r, 15] = chunks[STEPS][index]
            else:
                index = lax.rem(need_s[r, 0, x * 16 + lax.rem(z + 16 - step, 16)], 32)
                picked[r, 2 * step - 1] = chunks[step][0, index]
                index = lax.rem(need_s[r, 0, x * 16 + lax.rem(z + step, 16)], 32)
                picked[r, 2 * step] = chunks[step][1, index]

    def deliver(step):
        if step == 0:
            slots = pl.ds(0, 1)
        elif step == STEPS:
            slots = pl.ds(15, 1)
        else:
            slots = pl.ds(2 * step - 1, 2)

        @pl.loop(1, 32)
        def _(i):
            r = lax.rem(me + i, 32)
            pltpu.make_async_remote_copy(
                src_ref=picked.at[r, slots],
                dst_ref=out_ref.at[x, slots, part],
                send_sem=xy_send,
                recv_sem=xy_recv,
                device_id=reader(r),
                device_id_type=MESH,
            ).start()

        pltpu.make_async_copy(
            picked.at[me, slots], out_ref.at[x, slots, part], xy_recv
        ).start()

    own.wait()
    pair.wait_recv()
    forward(0)
    pltpu.make_async_copy(need_v, need_v, ask_recv).wait()
    table = pltpu.make_async_copy(need_v, need_s, smem_sem)
    table.start()
    table.wait()
    pick(0)
    deliver(0)
    for step in range(1, STEPS):
        forward(step)
        pick(step)
        deliver(step)
    hops[(STEPS - 1, 0, 0)].wait_recv()
    hops[(STEPS - 1, 1, 1)].wait_recv()
    pick(STEPS)
    deliver(STEPS)

    pair.wait_send()
    for one in hops.values():
        one.wait_send()
    asked = need_v.at[pl.ds(0, 31)]
    pltpu.make_async_copy(asked, asked, ask_send).wait()
    sent = picked.at[pl.ds(0, 31)]
    pltpu.make_async_copy(sent, sent, xy_send).wait()
    pltpu.make_async_copy(out_ref, out_ref, xy_recv).wait()


def gather_sources(embeddings, need):
    dma = pltpu.SemaphoreType.DMA
    one = pltpu.VMEM((32, 16, 128), jnp.bfloat16)
    two = pltpu.VMEM((2, 32, 16, 128), jnp.bfloat16)
    return pl.pallas_call(
        gather_kernel,
        out_shape=jax.ShapeDtypeStruct((4, 16, 8, 16, 128), jnp.bfloat16),
        in_specs=[pl.BlockSpec(memory_space=pl.ANY), pl.BlockSpec(memory_space=pl.ANY)],
        out_specs=pl.BlockSpec(memory_space=pltpu.VMEM),
        scratch_shapes=[
            one,
            *([two] * 7),
            one,
            pltpu.VMEM((32, 16, 16, 128), jnp.bfloat16),
            pltpu.VMEM((32, 1, 64), jnp.int32),
            pltpu.SMEM((32, 1, 64), jnp.int32),
            dma,
            dma,
            dma,
            dma((2, 8, 2)),
            dma((2, 8, 2)),
            dma,
            dma,
            dma,
            dma,
            dma,
        ],
        compiler_params=pltpu.CompilerParams(
            collective_id=0, has_side_effects=True, vmem_limit_bytes=16 * 2**20
        ),
        name="gather_sources",
    )(embeddings.reshape(16, 8, 16, 128), need)


GROUP = 16
TILES = 112


def spread_kernel(rows_ref, cols_ref, count_ref, src_ref, emb_ref, adj_ref, out_ref, tiles, acc, sems):
    z = place()[2]
    count = count_ref[0, 0]

    def load(g):
        span = pl.ds(g * GROUP, GROUP)
        return pltpu.make_async_copy(adj_ref.at[span], tiles.at[span], sems.at[g])

    for g in range(TILES // GROUP):
        load(g).start()
    acc[0:16] = emb_ref[...].astype(jnp.float32)

    def add(t):
        col = cols_ref[0, t]
        away = lax.rem(lax.rem(col, 16) - z + 16, 16)
        slot = jnp.where(away < 8, 2 * away, jnp.where(away == 8, 15, 31 - 2 * away))
        row = jnp.where(t < count, rows_ref[0, t], 16)
        product = jnp.dot(
            tiles[t], src_ref[(col // 16) * 16 + slot], preferred_element_type=jnp.float32
        )
        acc[row] += product

    for g in range(TILES // GROUP):
        load(g).wait()

        @pl.loop(0, GROUP // 4)
        def _(i):
            @pl.when(g * GROUP + i * 4 < count)
            def _():
                for j in range(4):
                    add(g * GROUP + i * 4 + j)

    out_ref[...] = acc[0:16].astype(jnp.bfloat16)


def spread_rows(rows, cols, count, sources, embeddings, adjacency):
    smem = pl.BlockSpec(memory_space=pltpu.SMEM)
    vmem = pl.BlockSpec(memory_space=pltpu.VMEM)
    return pl.pallas_call(
        spread_kernel,
        out_shape=jax.ShapeDtypeStruct((16, 128, 128), jnp.bfloat16),
        in_specs=[smem, smem, smem, vmem, vmem, pl.BlockSpec(memory_space=pl.ANY)],
        out_specs=vmem,
        scratch_shapes=[
            pltpu.VMEM((TILES, 128, 128), jnp.bfloat16),
            pltpu.VMEM((17, 128, 128), jnp.float32),
            pltpu.SemaphoreType.DMA((TILES // GROUP,)),
        ],
        compiler_params=pltpu.CompilerParams(vmem_limit_bytes=20 * 2**20),
        name="spread_rows",
    )(rows, cols, count, sources.reshape(64, 128, 128), embeddings.reshape(16, 128, 128), adjacency)


def laid_out(tiles, dim):
    lengths = list(tiles.shape[1:])
    lengths[dim] *= tiles.shape[0]
    return jnp.moveaxis(tiles, 0, dim).reshape(lengths)


def copy_for_each(value, axis):
    devices = lax.axis_size(axis)
    return lax.all_to_all(
        jnp.broadcast_to(value[None], (devices, *value.shape)), axis, 0, 0, tiled=True
    )


def collect(value, axis, dim):
    return laid_out(copy_for_each(value, axis), dim)


def merge_behaviors(behaviors, queries, w_query, w_key, w_value, w_out, mlp_gain, w_up, w_down):
    count_k, row_count, feature = behaviors.shape
    count_q = queries.shape[0]
    flat_keys = behaviors.reshape(count_k * row_count, feature)
    key_rows = jnp.dot(flat_keys, w_key, preferred_element_type=jnp.float32).reshape(
        count_k, row_count, HEADS, HEAD
    )
    value_rows = jnp.dot(flat_keys, w_value, preferred_element_type=jnp.float32).reshape(
        count_k, row_count, HEADS, HEAD
    )
    flat_queries = queries.reshape(count_q * row_count, feature)
    query_rows = jnp.dot(flat_queries, w_query, preferred_element_type=jnp.float32).reshape(
        count_q, row_count, HEADS, HEAD
    )
    scores = jnp.einsum(
        "qrhe,krhe->qrhk", query_rows, key_rows, precision=lax.Precision.HIGHEST
    ) / math.sqrt(HEAD)
    highest = jnp.max(scores, axis=-1, keepdims=True)
    weights = jnp.exp(scores - highest)
    weights = weights / jnp.sum(weights, axis=-1, keepdims=True)
    mixture = jnp.einsum("qrhk,krhe->qrhe", weights, value_rows, precision=lax.Precision.HIGHEST)
    mixture = mixture.reshape(count_q * row_count, feature).astype(jnp.bfloat16)
    residual = flat_queries.astype(jnp.float32) + jnp.dot(
        mixture, w_out, preferred_element_type=jnp.float32
    )
    meansq = jnp.mean(residual * residual, axis=-1, keepdims=True)
    normed = (residual * lax.rsqrt(meansq + 1e-06) * mlp_gain).astype(jnp.bfloat16)
    hidden = jax.nn.silu(jnp.dot(normed, w_up, preferred_element_type=jnp.float32)).astype(
        jnp.bfloat16
    )
    result = residual + jnp.dot(hidden, w_down, preferred_element_type=jnp.float32)
    return result.astype(jnp.bfloat16).reshape(count_q, row_count, feature)


def shards(
    embeddings,
    adjacency,
    tile_rows,
    tile_cols,
    tile_count,
    need_ids,
    w_query,
    w_key,
    w_value,
    w_out,
    mlp_gain,
    w_up,
    w_down,
):
    sources = gather_sources(embeddings, need_ids)
    spread = spread_rows(tile_rows, tile_cols, tile_count, sources, embeddings, adjacency[0])
    spread = spread.reshape(embeddings.shape)
    everyone = collect(spread[None], "beh", 0)
    index_now = lax.axis_index("beh")
    mine = lax.dynamic_slice_in_dim(everyone, index_now, 1, 0)
    return merge_behaviors(everyone, mine, w_query, w_key, w_value, w_out, mlp_gain, w_up, w_down)


def solution(mesh):
    in_specs = (
        P("node", None),
        P("beh", "node", None, None),
        P("beh", "node"),
        P("beh", "node"),
        P("beh", "node"),
        P("beh", "node"),
        P(),
        P(),
        P(),
        P(),
        P(),
        P(),
        P(),
    )
    out_specs = P("beh", "node", None)
    return jax.shard_map(shards, mesh=mesh, in_specs=in_specs, out_specs=out_specs, check_vma=False)
```

```python
import functools
import math

import jax
import jax.numpy as jnp
from jax import lax
from jax.experimental import pallas as pl
from jax.experimental.pallas import tpu as pltpu
from jax.sharding import PartitionSpec as P

HEAD = 32
MESH = pl.DeviceIdType.MESH
STEPS = 8


def place():
    y = lax.axis_index("beh")
    n = lax.axis_index("node")
    return n // 32, y, lax.rem(n // 2, 16), lax.rem(n, 2)


def device(x, y, z, k):
    return (y, (x * 16 + z) * 2 + k)


def gather_kernel(emb_ref, need_ref, out_ref, *scratch):
    chunks = scratch[:9]
    picked, need_v, need_s = scratch[9:12]
    own_sem, pair_send, pair_recv, ring_send, ring_recv = scratch[12:17]
    ask_send, ask_recv, smem_sem, xy_send, xy_recv = scratch[17:]
    x, y, z, k = place()
    me = x * 8 + y * 2 + k
    part = y * 2 + k
    above = device(x, y, lax.rem(z + 1, 16), k)
    below = device(x, y, lax.rem(z + 15, 16), k)
    twin = device(x, y, z, 1 - k)

    def reader(r):
        return device(r // 8, lax.rem(r, 8) // 2, z, lax.rem(r, 2))

    own = pltpu.make_async_copy(
        emb_ref.at[:, part], chunks[0].at[pl.ds(k * 16, 16)], own_sem
    )
    own.start()

    barrier = pltpu.get_barrier_semaphore()

    @pl.loop(1, 32)
    def _(i):
        pl.semaphore_signal(
            barrier, inc=1, device_id=reader(lax.rem(me + i, 32)), device_id_type=MESH
        )

    for neighbour in (above, below):
        pl.semaphore_signal(barrier, inc=1, device_id=neighbour, device_id_type=MESH)
    pl.semaphore_wait(barrier, 33)

    def half(step, way, h):
        blocks = pl.ds((k + h - 2 * k * h) * 16, 16)
        if step == 0 or step == STEPS:
            return chunks[step].at[blocks]
        return chunks[step].at[way, blocks]

    def hop(step, way, h):
        return pltpu.make_async_remote_copy(
            src_ref=half(step, way, h),
            dst_ref=half(step + 1, way, h),
            send_sem=ring_send.at[way, step, h],
            recv_sem=ring_recv.at[way, step, h],
            device_id=above if way == 0 else below,
            device_id_type=MESH,
        )

    hops = {}

    def forward(step, h):
        for way in range(2):
            if step > 0:
                hops[(step - 1, way, h)].wait_recv()
            if step < STEPS - 1 or way == h:
                hops[(step, way, h)] = hop(step, way, h)
                hops[(step, way, h)].start()

    def pick(step):
        @pl.loop(0, 32)
        def _(r):
            if step == 0:
                index = lax.rem(need_s[r, 0, x * 16 + z], 32)
                picked[r, 0] = chunks[0][index]
            elif step == STEPS:
                index = lax.rem(need_s[r, 0, x * 16 + lax.rem(z + 8, 16)], 32)
                picked[r, 15] = chunks[STEPS][index]
            else:
                index = lax.rem(need_s[r, 0, x * 16 + lax.rem(z + 16 - step, 16)], 32)
                picked[r, 2 * step - 1] = chunks[step][0, index]
                index = lax.rem(need_s[r, 0, x * 16 + lax.rem(z + step, 16)], 32)
                picked[r, 2 * step] = chunks[step][1, index]

    def deliver(step):
        if step == 0:
            slots = pl.ds(0, 1)
        elif step == STEPS:
            slots = pl.ds(15, 1)
        else:
            slots = pl.ds(2 * step - 1, 2)

        @pl.loop(1, 32)
        def _(i):
            r = lax.rem(me + i, 32)
            pltpu.make_async_remote_copy(
                src_ref=picked.at[r, slots],
                dst_ref=out_ref.at[x, slots, part],
                send_sem=xy_send,
                recv_sem=xy_recv,
                device_id=reader(r),
                device_id_type=MESH,
            ).start()

        pltpu.make_async_copy(
            picked.at[me, slots], out_ref.at[x, slots, part], xy_recv
        ).start()

    pair = pltpu.make_async_remote_copy(
        src_ref=emb_ref.at[:, y * 2 + 1 - k],
        dst_ref=chunks[0].at[pl.ds(k * 16, 16)],
        send_sem=pair_send,
        recv_sem=pair_recv,
        device_id=twin,
        device_id_type=MESH,
    )
    pair.start()

    own.wait()
    forward(0, 0)
    @pl.loop(1, 32)
    def _(i):
        pltpu.make_async_remote_copy(
            src_ref=need_ref,
            dst_ref=need_v.at[me],
            send_sem=ask_send,
            recv_sem=ask_recv,
            device_id=reader(lax.rem(me + i, 32)),
            device_id_type=MESH,
        ).start()

    pltpu.make_async_copy(need_ref, need_v.at[me], ask_recv).start()

    pair.wait_recv()
    forward(0, 1)
    forward(1, 0)
    pltpu.make_async_copy(need_v, need_v, ask_recv).wait()
    table = pltpu.make_async_copy(need_v, need_s, smem_sem)
    table.start()
    table.wait()
    pick(0)
    deliver(0)
    for step in range(1, STEPS):
        if step > 1:
            forward(step, 0)
        forward(step, 1)
        pick(step)
        deliver(step)
    hops[(STEPS - 1, 0, 0)].wait_recv()
    hops[(STEPS - 1, 1, 1)].wait_recv()
    pick(STEPS)
    deliver(STEPS)

    pair.wait_send()
    for one in hops.values():
        one.wait_send()
    asked = need_v.at[pl.ds(0, 31)]
    pltpu.make_async_copy(asked, asked, ask_send).wait()
    sent = picked.at[pl.ds(0, 31)]
    pltpu.make_async_copy(sent, sent, xy_send).wait()
    pltpu.make_async_copy(out_ref, out_ref, xy_recv).wait()


def gather_sources(embeddings, need):
    dma = pltpu.SemaphoreType.DMA
    one = pltpu.VMEM((32, 16, 128), jnp.bfloat16)
    two = pltpu.VMEM((2, 32, 16, 128), jnp.bfloat16)
    return pl.pallas_call(
        gather_kernel,
        out_shape=jax.ShapeDtypeStruct((4, 16, 8, 16, 128), jnp.bfloat16),
        in_specs=[pl.BlockSpec(memory_space=pltpu.HBM)] * 2,
        out_specs=pl.BlockSpec(memory_space=pltpu.VMEM),
        scratch_shapes=[
            one,
            *([two] * 7),
            one,
            pltpu.VMEM((32, 16, 16, 128), jnp.bfloat16),
            pltpu.VMEM((32, 1, 64), jnp.int32),
            pltpu.SMEM((32, 1, 64), jnp.int32),
            dma,
            dma,
            dma,
            dma((2, 8, 2)),
            dma((2, 8, 2)),
            dma,
            dma,
            dma,
            dma,
            dma,
        ],
        compiler_params=pltpu.CompilerParams(
            collective_id=0, has_side_effects=True, vmem_limit_bytes=16 * 2**20
        ),
        cost_estimate=pl.CostEstimate(
            flops=2**33, transcendentals=0, bytes_accessed=2**26
        ),
        name="gather_sources",
    )(
        pltpu.with_memory_space_constraint(embeddings.reshape(16, 8, 16, 128), pltpu.HBM),
        pltpu.with_memory_space_constraint(need, pltpu.HBM),
    )


GROUP = 4
TILES = 112


def spread_kernel(rows_ref, cols_ref, count_ref, src_ref, emb_ref, adj_ref, out_ref, acc):
    z = place()[2]
    count = count_ref[0, 0]

    acc[0:16] = emb_ref[...].astype(jnp.float32)

    def add(t):
        col = cols_ref[0, t]
        away = lax.rem(lax.rem(col, 16) - z + 16, 16)
        slot = jnp.where(away < 8, 2 * away, jnp.where(away == 8, 15, 31 - 2 * away))
        row = jnp.where(t < count, rows_ref[0, t], 16)
        product = jnp.dot(
            adj_ref[t], src_ref[(col // 16) * 16 + slot], preferred_element_type=jnp.float32
        )
        acc[row] += product

    @pl.loop(0, (count + GROUP - 1) // GROUP)
    def _(i):
        for j in range(GROUP):
            add(i * GROUP + j)

    out_ref[...] = acc[0:16].astype(jnp.bfloat16)


def spread_rows(rows, cols, count, sources, embeddings, adjacency):
    smem = pl.BlockSpec(memory_space=pltpu.SMEM)
    vmem = pl.BlockSpec(memory_space=pltpu.VMEM)
    return pl.pallas_call(
        spread_kernel,
        out_shape=jax.ShapeDtypeStruct((16, 128, 128), jnp.bfloat16),
        in_specs=[smem, smem, smem, vmem, vmem, vmem],
        out_specs=vmem,
        scratch_shapes=[
            pltpu.VMEM((17, 128, 128), jnp.float32),
        ],
        compiler_params=pltpu.CompilerParams(vmem_limit_bytes=20 * 2**20),
        name="spread_rows",
    )(rows, cols, count, sources.reshape(64, 128, 128), embeddings.reshape(16, 128, 128), adjacency)


CHUNKS = 4
ROWS = 512 // CHUNKS


def merge_kernel(
    spread_ref,
    wq_ref,
    wk_ref,
    wv_ref,
    wo_ref,
    gain_ref,
    up_ref,
    down_ref,
    out_ref,
    got,
    done,
    own_sem,
    in_send,
    in_recv,
    out_send,
    out_recv,
):
    x, y, z, k = place()
    own = pltpu.make_async_copy(spread_ref.at[y], got.at[y], own_sem)
    own.start()
    barrier = pltpu.get_barrier_semaphore()
    for i in range(1, 4):
        pl.semaphore_signal(
            barrier, inc=1, device_id=device(x, lax.rem(y + i, 4), z, k), device_id_type=MESH
        )
    pl.semaphore_wait(barrier, 3)

    @pl.loop(0, CHUNKS)
    def _(c):
        span = pl.ds(pl.multiple_of(c * ROWS, ROWS), ROWS)
        for i in range(1, 4):
            there = lax.rem(y + i, 4)
            pltpu.make_async_remote_copy(
                src_ref=spread_ref.at[there, span],
                dst_ref=got.at[y, span],
                send_sem=in_send,
                recv_sem=in_recv.at[c],
                device_id=device(x, there, z, k),
                device_id_type=MESH,
            ).start()

    lane = lax.broadcasted_iota(jnp.int32, (128, 128), 0) // HEAD
    same = (lane == lax.broadcasted_iota(jnp.int32, (128, 128), 1) // HEAD).astype(jnp.bfloat16)
    own.wait()

    @pl.loop(0, CHUNKS)
    def _(c):
        span = pl.ds(pl.multiple_of(c * ROWS, ROWS), ROWS)
        arrived = got.at[pl.ds(0, 3), span]
        pltpu.make_async_copy(arrived, arrived, in_recv.at[c]).wait()
        flat = got[:, span, :].reshape(4 * ROWS, 128)
        query = jnp.dot(flat, wq_ref[...], preferred_element_type=jnp.float32)
        query = query * (math.log2(math.e) / math.sqrt(HEAD))
        key = jnp.dot(flat, wk_ref[...], preferred_element_type=jnp.float32)
        value = jnp.dot(flat, wv_ref[...], preferred_element_type=jnp.float32)
        mixed = []
        for q in range(4):
            mine = query[q * ROWS : (q + 1) * ROWS]
            scores = []
            for b in range(4):
                part = mine * key[b * ROWS : (b + 1) * ROWS]
                high = part.astype(jnp.bfloat16)
                low = (part - high.astype(jnp.float32)).astype(jnp.bfloat16)
                scores.append(
                    jnp.dot(high, same, preferred_element_type=jnp.float32)
                    + jnp.dot(low, same, preferred_element_type=jnp.float32)
                )
            top = jnp.maximum(
                jnp.maximum(scores[0], scores[1]), jnp.maximum(scores[2], scores[3])
            )
            weights = [jnp.exp2(s - top) for s in scores]
            total = (weights[0] + weights[1]) + (weights[2] + weights[3])
            blend = weights[0] * value[:ROWS]
            for b in range(1, 4):
                blend = blend + weights[b] * value[b * ROWS : (b + 1) * ROWS]
            mixed.append((blend / total).astype(jnp.bfloat16))
        mixture = jnp.concatenate(mixed, axis=0)
        residual = flat.astype(jnp.float32) + jnp.dot(
            mixture, wo_ref[...], preferred_element_type=jnp.float32
        )
        meansq = jnp.mean(residual * residual, axis=-1, keepdims=True)
        normed = (residual * lax.rsqrt(meansq + 1e-06) * gain_ref[...]).astype(jnp.bfloat16)
        hidden = jax.nn.silu(
            jnp.dot(normed, up_ref[...], preferred_element_type=jnp.float32)
        ).astype(jnp.bfloat16)
        result = residual + jnp.dot(hidden, down_ref[...], preferred_element_type=jnp.float32)
        done[:, span, :] = result.astype(jnp.bfloat16).reshape(4, ROWS, 128)
        for i in range(1, 4):
            there = lax.rem(y + i, 4)
            pltpu.make_async_remote_copy(
                src_ref=done.at[there, span],
                dst_ref=out_ref.at[y, span],
                send_sem=out_send,
                recv_sem=out_recv,
                device_id=device(x, there, z, k),
                device_id_type=MESH,
            ).start()

    own = pltpu.make_async_copy(done.at[y], out_ref.at[y], own_sem)
    own.start()
    own.wait()
    three = got.at[pl.ds(0, 3)]
    pltpu.make_async_copy(three, three, in_send).wait()
    pltpu.make_async_copy(three, three, out_send).wait()
    pltpu.make_async_copy(three, three, out_recv).wait()


def merge_rows(spread, w_query, w_key, w_value, w_out, mlp_gain, w_up, w_down):
    dma = pltpu.SemaphoreType.DMA
    vmem = pl.BlockSpec(memory_space=pltpu.VMEM)
    quarters = (4, 512, 128)
    return pl.pallas_call(
        merge_kernel,
        out_shape=jax.ShapeDtypeStruct(quarters, jnp.bfloat16),
        in_specs=[vmem] * 8,
        out_specs=vmem,
        scratch_shapes=[
            pltpu.VMEM(quarters, jnp.bfloat16),
            pltpu.VMEM(quarters, jnp.bfloat16),
            dma,
            dma,
            dma((CHUNKS,)),
            dma,
            dma,
        ],
        compiler_params=pltpu.CompilerParams(
            collective_id=1, has_side_effects=True, vmem_limit_bytes=24 * 2**20
        ),
        name="merge_rows",
    )(
        spread.reshape(quarters),
        w_query,
        w_key,
        w_value,
        w_out,
        mlp_gain.reshape(1, 128),
        w_up,
        w_down,
    )


def shards(
    embeddings,
    adjacency,
    tile_rows,
    tile_cols,
    tile_count,
    need_ids,
    w_query,
    w_key,
    w_value,
    w_out,
    mlp_gain,
    w_up,
    w_down,
):
    sources = gather_sources(embeddings, need_ids)
    spread = spread_rows(tile_rows, tile_cols, tile_count, sources, embeddings, adjacency[0])
    merged = merge_rows(spread, w_query, w_key, w_value, w_out, mlp_gain, w_up, w_down)
    return merged.reshape(1, *embeddings.shape)


def solution(mesh):
    in_specs = (
        P("node", None),
        P("beh", "node", None, None),
        P("beh", "node"),
        P("beh", "node"),
        P("beh", "node"),
        P("beh", "node"),
        P(),
        P(),
        P(),
        P(),
        P(),
        P(),
        P(),
    )
    out_specs = P("beh", "node", None)
    return jax.shard_map(shards, mesh=mesh, in_specs=in_specs, out_specs=out_specs, check_vma=False)
```

```python
import functools
import math

import jax
import jax.numpy as jnp
from jax import lax
from jax.experimental import pallas as pl
from jax.experimental.pallas import tpu as pltpu
from jax.sharding import PartitionSpec as P

HEAD = 32
MESH = pl.DeviceIdType.MESH
STEPS = 8
FAR_FIRST = sorted(
    ((i, j) for i in range(4) for j in range(8) if i or j),
    key=lambda at: -(min(at[0], 4 - at[0]) * 2 + min(at[1], 8 - at[1])),
)


def place():
    y = lax.axis_index("beh")
    n = lax.axis_index("node")
    return n // 32, y, lax.rem(n // 2, 16), lax.rem(n, 2)


def device(x, y, z, k):
    return (y, (x * 16 + z) * 2 + k)


def gather_kernel(emb_ref, need_ref, out_ref, *scratch):
    chunks = scratch[:9]
    picked, mid, need_x, need_v, need_s = scratch[9:14]
    own_sem, pair_send, pair_recv, ring_send, ring_recv = scratch[14:19]
    ask_send, ask_recv, smem_sem, x_send, x_recv, y_send, y_recv = scratch[19:]
    x, y, z, k = place()
    part = y * 2 + k
    above = device(x, y, lax.rem(z + 1, 16), k)
    below = device(x, y, lax.rem(z + 15, 16), k)
    twin = device(x, y, z, 1 - k)
    rows = [lax.rem(x + i, 4) for i in range(4)]
    parts = [lax.rem(part + i, 8) for i in range(8)]
    row_peers = [device(xx, y, z, k) for xx in rows]
    part_peers = [device(x, p // 2, z, lax.rem(p, 2)) for p in parts]

    def send(src, dst, sent, landed, where):
        copy = pltpu.make_async_remote_copy(
            src_ref=src,
            dst_ref=dst,
            send_sem=sent,
            recv_sem=landed,
            device_id=where,
            device_id_type=MESH,
        )
        copy.start()
        return copy

    def wait_bytes(ref, sem):
        pltpu.make_async_copy(ref, ref, sem).wait()

    own = pltpu.make_async_copy(
        emb_ref.at[:, part], chunks[0].at[pl.ds(k * 16, 16)], own_sem
    )
    own.start()
    pltpu.make_async_copy(need_ref, need_x.at[x], ask_recv.at[0]).start()

    barrier = pltpu.get_barrier_semaphore()
    for peer in (above, below, *row_peers[1:], *part_peers[1:]):
        pl.semaphore_signal(barrier, inc=1, device_id=peer, device_id_type=MESH)
    pl.semaphore_wait(barrier, 12)

    def half(step, way, h):
        core = k if h < 2 else 1 - k
        blocks = pl.ds(core * 16 + (h % 2) * 8, 8)
        if step == 0 or step == STEPS:
            return chunks[step].at[blocks]
        return chunks[step].at[way, blocks]

    hops = {}

    def forward(step, h):
        for way in range(2):
            if (step - 1, way, h) in hops:
                hops[(step - 1, way, h)].wait_recv()
            if step < STEPS - 1 or (step < STEPS and way == h % 2):
                hops[(step, way, h)] = send(
                    half(step, way, h),
                    half(step + 1, way, h),
                    ring_send.at[way, step, h],
                    ring_recv.at[way, step, h],
                    above if way == 0 else below,
                )

    def third(step):
        return 0 if step == 0 else 2 if step == STEPS else 1

    def pick(step, low=0, high=8):
        @pl.loop(low, high)
        def _(p):
            for xx in range(4):
                if step == 0:
                    index = lax.rem(need_s[p, xx, 0, x * 16 + z], 32)
                    picked[0, xx * 8 + p, 0] = chunks[0][index]
                elif step == STEPS:
                    index = lax.rem(need_s[p, xx, 0, x * 16 + lax.rem(z + 8, 16)], 32)
                    picked[STEPS, xx * 8 + p, 0] = chunks[STEPS][index]
                else:
                    index = lax.rem(need_s[p, xx, 0, x * 16 + lax.rem(z + 16 - step, 16)], 32)
                    picked[step, xx * 8 + p, 0] = chunks[step][0, index]
                    index = lax.rem(need_s[p, xx, 0, x * 16 + lax.rem(z + step, 16)], 32)
                    picked[step, xx * 8 + p, 1] = chunks[step][1, index]

    me = x * 8 + part

    def deliver(step):
        width = pl.ds(0, 1 if step == 0 or step == STEPS else 2)
        turn = third(step)
        pltpu.make_async_copy(
            picked.at[step, me, width], out_ref.at[step, part, x, width], y_recv.at[turn]
        ).start()
        for i, j in FAR_FIRST:
            send(
                picked.at[step, rows[i] * 8 + parts[j], width],
                out_ref.at[step, part, x, width],
                y_send.at[turn],
                y_recv.at[turn],
                device(rows[i], parts[j] // 2, z, lax.rem(parts[j], 2)),
            )

    for peer in row_peers[1:]:
        send(need_ref, need_x.at[x], ask_send.at[0], ask_recv.at[0], peer)
    pair = send(
        emb_ref.at[:, y * 2 + 1 - k],
        chunks[0].at[pl.ds(k * 16, 16)],
        pair_send,
        pair_recv,
        twin,
    )
    own.wait()
    forward(0, 0)
    forward(0, 1)
    wait_bytes(need_x, ask_recv.at[0])
    for peer in part_peers[1:]:
        send(need_x, need_v.at[part], ask_send.at[1], ask_recv.at[1], peer)
    pltpu.make_async_copy(need_x, need_v.at[part], ask_recv.at[1]).start()
    pair.wait_recv()
    forward(0, 2)
    forward(0, 3)
    forward(1, 0)
    forward(1, 1)
    wait_bytes(need_v, ask_recv.at[1])
    table = pltpu.make_async_copy(need_v, need_s, smem_sem)
    table.start()
    forward(1, 2)
    table.wait()
    forward(1, 3)
    pick(0)
    deliver(0)
    pick(1)
    deliver(1)
    for step in range(2, STEPS + 1):
        for h in range(4):
            forward(step, h)
        pick(step)
        deliver(step)

    pair.wait_send()
    for one in hops.values():
        one.wait_send()
    wait_bytes(need_x.at[pl.ds(0, 3)], ask_send.at[0])
    wait_bytes(need_v.at[pl.ds(0, 7)], ask_send.at[1])
    ends = ((0, pl.ds(0, 1), pl.ds(0, 1)), (1, pl.ds(1, 7), pl.ds(0, 2)), (2, pl.ds(8, 1), pl.ds(0, 1)))
    for turn, steps, width in ends:
        wait_bytes(picked.at[steps, pl.ds(0, 31), width], y_send.at[turn])
        wait_bytes(out_ref.at[steps, :, :, width], y_recv.at[turn])


def gather_sources(embeddings, need):
    dma = pltpu.SemaphoreType.DMA
    one = pltpu.VMEM((32, 16, 128), jnp.bfloat16)
    two = pltpu.VMEM((2, 32, 16, 128), jnp.bfloat16)
    picks = pltpu.VMEM((9, 32, 2, 16, 128), jnp.bfloat16)
    return pl.pallas_call(
        gather_kernel,
        out_shape=jax.ShapeDtypeStruct((9, 8, 4, 2, 16, 128), jnp.bfloat16),
        in_specs=[pl.BlockSpec(memory_space=pltpu.HBM)] * 2,
        out_specs=pl.BlockSpec(memory_space=pltpu.VMEM),
        scratch_shapes=[
            one,
            *([two] * 7),
            one,
            picks,
            pltpu.VMEM((8, 128), jnp.float32),
            pltpu.VMEM((4, 1, 64), jnp.int32),
            pltpu.VMEM((8, 4, 1, 64), jnp.int32),
            pltpu.SMEM((8, 4, 1, 64), jnp.int32),
            dma,
            dma,
            dma,
            dma((2, 8, 4)),
            dma((2, 8, 4)),
            dma((2,)),
            dma((2,)),
            dma,
            dma((3,)),
            dma((9,)),
            dma((3,)),
            dma((3,)),
        ],
        compiler_params=pltpu.CompilerParams(
            collective_id=0, has_side_effects=True, vmem_limit_bytes=16 * 2**20
        ),
        cost_estimate=pl.CostEstimate(
            flops=2**33, transcendentals=0, bytes_accessed=2**26
        ),
        name="gather_sources",
    )(
        pltpu.with_memory_space_constraint(embeddings.reshape(16, 8, 16, 128), pltpu.HBM),
        pltpu.with_memory_space_constraint(need, pltpu.HBM),
    )


GROUP = 4
TILES = 112


def spread_kernel(rows_ref, cols_ref, count_ref, src_ref, emb_ref, adj_ref, out_ref, acc):
    z = place()[2]
    count = count_ref[0, 0]

    acc[0:16] = emb_ref[...].astype(jnp.float32)

    def add(t):
        col = cols_ref[0, t]
        away = lax.rem(lax.rem(col, 16) - z + 16, 16)
        step = jnp.minimum(away, 16 - away)
        way = jnp.where((away > 0) & (away < 8), 1, 0)
        row = jnp.where(t < count, rows_ref[0, t], 16)
        product = jnp.dot(
            adj_ref[t], src_ref[step, :, col // 16, way].reshape(128, 128), preferred_element_type=jnp.float32
        )
        acc[row] += product

    @pl.loop(0, (count + GROUP - 1) // GROUP)
    def _(i):
        for j in range(GROUP):
            add(i * GROUP + j)

    out_ref[...] = acc[0:16].astype(jnp.bfloat16)


def spread_rows(rows, cols, count, sources, embeddings, adjacency):
    smem = pl.BlockSpec(memory_space=pltpu.SMEM)
    vmem = pl.BlockSpec(memory_space=pltpu.VMEM)
    return pl.pallas_call(
        spread_kernel,
        out_shape=jax.ShapeDtypeStruct((16, 128, 128), jnp.bfloat16),
        in_specs=[smem, smem, smem, vmem, vmem, vmem],
        out_specs=vmem,
        scratch_shapes=[
            pltpu.VMEM((17, 128, 128), jnp.float32),
        ],
        compiler_params=pltpu.CompilerParams(vmem_limit_bytes=20 * 2**20),
        name="spread_rows",
    )(rows, cols, count, sources, embeddings.reshape(16, 128, 128), adjacency)


CHUNKS = 4
ROWS = 512 // CHUNKS


def merge_kernel(
    spread_ref,
    wq_ref,
    wk_ref,
    wv_ref,
    wo_ref,
    gain_ref,
    up_ref,
    down_ref,
    out_ref,
    got,
    done,
    own_sem,
    in_send,
    in_recv,
    out_send,
    out_recv,
):
    x, y, z, k = place()
    own = pltpu.make_async_copy(spread_ref.at[y], got.at[y], own_sem)
    own.start()
    barrier = pltpu.get_barrier_semaphore()
    for i in range(1, 4):
        pl.semaphore_signal(
            barrier, inc=1, device_id=device(x, lax.rem(y + i, 4), z, k), device_id_type=MESH
        )
    pl.semaphore_wait(barrier, 3)

    @pl.loop(0, CHUNKS)
    def _(c):
        span = pl.ds(pl.multiple_of(c * ROWS, ROWS), ROWS)
        for i in range(1, 4):
            there = lax.rem(y + i, 4)
            pltpu.make_async_remote_copy(
                src_ref=spread_ref.at[there, span],
                dst_ref=got.at[y, span],
                send_sem=in_send,
                recv_sem=in_recv.at[c],
                device_id=device(x, there, z, k),
                device_id_type=MESH,
            ).start()

    lane = lax.broadcasted_iota(jnp.int32, (128, 128), 0) // HEAD
    same = (lane == lax.broadcasted_iota(jnp.int32, (128, 128), 1) // HEAD).astype(jnp.bfloat16)
    own.wait()

    @pl.loop(0, CHUNKS)
    def _(c):
        span = pl.ds(pl.multiple_of(c * ROWS, ROWS), ROWS)
        arrived = got.at[pl.ds(0, 3), span]
        pltpu.make_async_copy(arrived, arrived, in_recv.at[c]).wait()
        flat = got[:, span, :].reshape(4 * ROWS, 128)
        query = jnp.dot(flat, wq_ref[...], preferred_element_type=jnp.float32)
        query = query * (math.log2(math.e) / math.sqrt(HEAD))
        key = jnp.dot(flat, wk_ref[...], preferred_element_type=jnp.float32)
        value = jnp.dot(flat, wv_ref[...], preferred_element_type=jnp.float32)
        mixed = []
        for q in range(4):
            mine = query[q * ROWS : (q + 1) * ROWS]
            scores = []
            for b in range(4):
                part = mine * key[b * ROWS : (b + 1) * ROWS]
                high = part.astype(jnp.bfloat16)
                low = (part - high.astype(jnp.float32)).astype(jnp.bfloat16)
                scores.append(
                    jnp.dot(high, same, preferred_element_type=jnp.float32)
                    + jnp.dot(low, same, preferred_element_type=jnp.float32)
                )
            top = jnp.maximum(
                jnp.maximum(scores[0], scores[1]), jnp.maximum(scores[2], scores[3])
            )
            weights = [jnp.exp2(s - top) for s in scores]
            total = (weights[0] + weights[1]) + (weights[2] + weights[3])
            blend = weights[0] * value[:ROWS]
            for b in range(1, 4):
                blend = blend + weights[b] * value[b * ROWS : (b + 1) * ROWS]
            mixed.append((blend / total).astype(jnp.bfloat16))
        mixture = jnp.concatenate(mixed, axis=0)
        residual = flat.astype(jnp.float32) + jnp.dot(
            mixture, wo_ref[...], preferred_element_type=jnp.float32
        )
        meansq = jnp.mean(residual * residual, axis=-1, keepdims=True)
        normed = (residual * lax.rsqrt(meansq + 1e-06) * gain_ref[...]).astype(jnp.bfloat16)
        hidden = jax.nn.silu(
            jnp.dot(normed, up_ref[...], preferred_element_type=jnp.float32)
        ).astype(jnp.bfloat16)
        result = residual + jnp.dot(hidden, down_ref[...], preferred_element_type=jnp.float32)
        done[:, span, :] = result.astype(jnp.bfloat16).reshape(4, ROWS, 128)
        for i in range(1, 4):
            there = lax.rem(y + i, 4)
            pltpu.make_async_remote_copy(
                src_ref=done.at[there, span],
                dst_ref=out_ref.at[y, span],
                send_sem=out_send,
                recv_sem=out_recv,
                device_id=device(x, there, z, k),
                device_id_type=MESH,
            ).start()

    own = pltpu.make_async_copy(done.at[y], out_ref.at[y], own_sem)
    own.start()
    own.wait()
    three = got.at[pl.ds(0, 3)]
    pltpu.make_async_copy(three, three, in_send).wait()
    pltpu.make_async_copy(three, three, out_send).wait()
    pltpu.make_async_copy(three, three, out_recv).wait()


def merge_rows(spread, w_query, w_key, w_value, w_out, mlp_gain, w_up, w_down):
    dma = pltpu.SemaphoreType.DMA
    vmem = pl.BlockSpec(memory_space=pltpu.VMEM)
    quarters = (4, 512, 128)
    return pl.pallas_call(
        merge_kernel,
        out_shape=jax.ShapeDtypeStruct(quarters, jnp.bfloat16),
        in_specs=[vmem] * 8,
        out_specs=vmem,
        scratch_shapes=[
            pltpu.VMEM(quarters, jnp.bfloat16),
            pltpu.VMEM(quarters, jnp.bfloat16),
            dma,
            dma,
            dma((CHUNKS,)),
            dma,
            dma,
        ],
        compiler_params=pltpu.CompilerParams(
            collective_id=1, has_side_effects=True, vmem_limit_bytes=24 * 2**20
        ),
        name="merge_rows",
    )(
        spread.reshape(quarters),
        w_query,
        w_key,
        w_value,
        w_out,
        mlp_gain.reshape(1, 128),
        w_up,
        w_down,
    )


def shards(
    embeddings,
    adjacency,
    tile_rows,
    tile_cols,
    tile_count,
    need_ids,
    w_query,
    w_key,
    w_value,
    w_out,
    mlp_gain,
    w_up,
    w_down,
):
    sources = gather_sources(embeddings, need_ids)
    spread = spread_rows(tile_rows, tile_cols, tile_count, sources, embeddings, adjacency[0])
    merged = merge_rows(spread, w_query, w_key, w_value, w_out, mlp_gain, w_up, w_down)
    return merged.reshape(1, *embeddings.shape)


def solution(mesh):
    in_specs = (
        P("node", None),
        P("beh", "node", None, None),
        P("beh", "node"),
        P("beh", "node"),
        P("beh", "node"),
        P("beh", "node"),
        P(),
        P(),
        P(),
        P(),
        P(),
        P(),
        P(),
    )
    out_specs = P("beh", "node", None)
    return jax.shard_map(shards, mesh=mesh, in_specs=in_specs, out_specs=out_specs, check_vma=False)
```

```python
import functools
import math

import jax
import jax.numpy as jnp
from jax import lax
from jax.experimental import pallas as pl
from jax.experimental.pallas import tpu as pltpu
from jax.sharding import PartitionSpec as P

HEAD = 32
MESH = pl.DeviceIdType.MESH
STEPS = 8
FAR_FIRST = sorted(
    ((i, j) for i in range(4) for j in range(8) if i or j),
    key=lambda at: -(min(at[0], 4 - at[0]) * 2 + min(at[1], 8 - at[1])),
)


def place():
    y = lax.axis_index("beh")
    n = lax.axis_index("node")
    return n // 32, y, lax.rem(n // 2, 16), lax.rem(n, 2)


def device(x, y, z, k):
    return (y, (x * 16 + z) * 2 + k)


def gather_kernel(emb_ref, need_ref, out_ref, *scratch):
    chunks = scratch[:9]
    picked, mid, need_x, need_v, need_s = scratch[9:14]
    own_sem, pair_send, pair_recv, ring_send, ring_recv = scratch[14:19]
    ask_send, ask_recv, smem_sem, x_send, x_recv, y_send, y_recv = scratch[19:]
    x, y, z, k = place()
    part = y * 2 + k
    above = device(x, y, lax.rem(z + 1, 16), k)
    below = device(x, y, lax.rem(z + 15, 16), k)
    twin = device(x, y, z, 1 - k)
    rows = [lax.rem(x + i, 4) for i in range(4)]
    parts = [lax.rem(part + i, 8) for i in range(8)]
    row_peers = [device(xx, y, z, k) for xx in rows]
    part_peers = [device(x, p // 2, z, lax.rem(p, 2)) for p in parts]

    def send(src, dst, sent, landed, where):
        copy = pltpu.make_async_remote_copy(
            src_ref=src,
            dst_ref=dst,
            send_sem=sent,
            recv_sem=landed,
            device_id=where,
            device_id_type=MESH,
        )
        copy.start()
        return copy

    def wait_bytes(ref, sem):
        pltpu.make_async_copy(ref, ref, sem).wait()

    own = pltpu.make_async_copy(
        emb_ref.at[:, part], chunks[0].at[pl.ds(k * 16, 16)], own_sem
    )
    own.start()
    pltpu.make_async_copy(need_ref, need_x.at[x], ask_recv.at[0]).start()

    barrier = pltpu.get_barrier_semaphore()
    for peer in (above, below, *row_peers[1:], *part_peers[1:]):
        pl.semaphore_signal(barrier, inc=1, device_id=peer, device_id_type=MESH)
    pl.semaphore_wait(barrier, 12)

    def half(step, way, h):
        core = k if h < 2 else 1 - k
        blocks = pl.ds(core * 16 + (h % 2) * 8, 8)
        if step == 0 or step == STEPS:
            return chunks[step].at[blocks]
        return chunks[step].at[way, blocks]

    hops = {}

    def forward(step, h):
        for way in range(2):
            if (step - 1, way, h) in hops:
                hops[(step - 1, way, h)].wait_recv()
            if step < STEPS - 1 or (step < STEPS and way == h % 2):
                hops[(step, way, h)] = send(
                    half(step, way, h),
                    half(step + 1, way, h),
                    ring_send.at[way, step, h],
                    ring_recv.at[way, step, h],
                    above if way == 0 else below,
                )

    def third(step):
        return 0 if step == 0 else 2 if step == STEPS else 1

    def pick(step, low=0, high=8):
        @pl.loop(low, high)
        def _(p):
            for xx in range(4):
                if step == 0:
                    index = lax.rem(need_s[p, xx, 0, x * 16 + z], 32)
                    picked[0, xx * 8 + p, 0] = chunks[0][index]
                elif step == STEPS:
                    index = lax.rem(need_s[p, xx, 0, x * 16 + lax.rem(z + 8, 16)], 32)
                    picked[STEPS, xx * 8 + p, 0] = chunks[STEPS][index]
                else:
                    index = lax.rem(need_s[p, xx, 0, x * 16 + lax.rem(z + 16 - step, 16)], 32)
                    picked[step, xx * 8 + p, 0] = chunks[step][0, index]
                    index = lax.rem(need_s[p, xx, 0, x * 16 + lax.rem(z + step, 16)], 32)
                    picked[step, xx * 8 + p, 1] = chunks[step][1, index]

    me = x * 8 + part

    def deliver(step):
        width = pl.ds(0, 1 if step == 0 or step == STEPS else 2)
        turn = third(step)
        pltpu.make_async_copy(
            picked.at[step, me, width], out_ref.at[step, part, x, width], y_recv.at[turn]
        ).start()
        for i, j in FAR_FIRST:
            send(
                picked.at[step, rows[i] * 8 + parts[j], width],
                out_ref.at[step, part, x, width],
                y_send.at[turn],
                y_recv.at[turn],
                device(rows[i], parts[j] // 2, z, lax.rem(parts[j], 2)),
            )

    for peer in row_peers[1:]:
        send(need_ref, need_x.at[x], ask_send.at[0], ask_recv.at[0], peer)
    pair = send(
        emb_ref.at[:, y * 2 + 1 - k],
        chunks[0].at[pl.ds(k * 16, 16)],
        pair_send,
        pair_recv,
        twin,
    )
    own.wait()
    forward(0, 0)
    forward(0, 1)
    wait_bytes(need_x, ask_recv.at[0])
    for peer in part_peers[1:]:
        send(need_x, need_v.at[part], ask_send.at[1], ask_recv.at[1], peer)
    pltpu.make_async_copy(need_x, need_v.at[part], ask_recv.at[1]).start()
    pair.wait_recv()
    forward(0, 2)
    forward(0, 3)
    forward(1, 0)
    forward(1, 1)
    wait_bytes(need_v, ask_recv.at[1])
    table = pltpu.make_async_copy(need_v, need_s, smem_sem)
    table.start()
    forward(1, 2)
    table.wait()
    forward(1, 3)
    pick(0)
    deliver(0)
    pick(1)
    deliver(1)
    for step in range(2, STEPS + 1):
        for h in range(4):
            forward(step, h)
        pick(step)
        deliver(step)

    pair.wait_send()
    for one in hops.values():
        one.wait_send()
    wait_bytes(need_x.at[pl.ds(0, 3)], ask_send.at[0])
    wait_bytes(need_v.at[pl.ds(0, 7)], ask_send.at[1])
    ends = ((0, pl.ds(0, 1), pl.ds(0, 1)), (1, pl.ds(1, 7), pl.ds(0, 2)), (2, pl.ds(8, 1), pl.ds(0, 1)))
    for turn, steps, width in ends:
        wait_bytes(picked.at[steps, pl.ds(0, 31), width], y_send.at[turn])
        wait_bytes(out_ref.at[steps, :, :, width], y_recv.at[turn])


def gather_sources(embeddings, need):
    dma = pltpu.SemaphoreType.DMA
    one = pltpu.VMEM((32, 16, 128), jnp.bfloat16)
    two = pltpu.VMEM((2, 32, 16, 128), jnp.bfloat16)
    picks = pltpu.VMEM((9, 32, 2, 16, 128), jnp.bfloat16)
    return pl.pallas_call(
        gather_kernel,
        out_shape=jax.ShapeDtypeStruct((9, 8, 4, 2, 16, 128), jnp.bfloat16),
        in_specs=[pl.BlockSpec(memory_space=pltpu.HBM)] * 2,
        out_specs=pl.BlockSpec(memory_space=pltpu.VMEM),
        scratch_shapes=[
            one,
            *([two] * 7),
            one,
            picks,
            pltpu.VMEM((8, 128), jnp.float32),
            pltpu.VMEM((4, 1, 64), jnp.int32),
            pltpu.VMEM((8, 4, 1, 64), jnp.int32),
            pltpu.SMEM((8, 4, 1, 64), jnp.int32),
            dma,
            dma,
            dma,
            dma((2, 8, 4)),
            dma((2, 8, 4)),
            dma((2,)),
            dma((2,)),
            dma,
            dma((3,)),
            dma((9,)),
            dma((3,)),
            dma((3,)),
        ],
        compiler_params=pltpu.CompilerParams(
            collective_id=0, has_side_effects=True, vmem_limit_bytes=16 * 2**20
        ),
        cost_estimate=pl.CostEstimate(
            flops=2**33, transcendentals=0, bytes_accessed=2**26
        ),
        name="gather_sources",
    )(
        pltpu.with_memory_space_constraint(embeddings.reshape(16, 8, 16, 128), pltpu.HBM),
        pltpu.with_memory_space_constraint(need, pltpu.HBM),
    )


GROUP = 16
TILES = 112


def spread_kernel(rows_ref, cols_ref, count_ref, src_ref, emb_ref, adj_ref, out_ref, acc):
    z = place()[2]
    count = count_ref[0, 0]

    acc[0:16] = emb_ref[...].astype(jnp.float32)

    def add(t):
        col = cols_ref[0, t]
        away = lax.rem(lax.rem(col, 16) - z + 16, 16)
        step = jnp.minimum(away, 16 - away)
        way = jnp.where((away > 0) & (away < 8), 1, 0)
        row = jnp.where(t < count, rows_ref[0, t], 16)
        product = jnp.dot(
            adj_ref[t], src_ref[step, :, col // 16, way].reshape(128, 128), preferred_element_type=jnp.float32
        )
        acc[row] += product

    @pl.loop(0, (count + GROUP - 1) // GROUP)
    def _(i):
        for j in range(GROUP):
            add(i * GROUP + j)

    out_ref[...] = acc[0:16].astype(jnp.bfloat16)


def spread_rows(rows, cols, count, sources, embeddings, adjacency):
    smem = pl.BlockSpec(memory_space=pltpu.SMEM)
    vmem = pl.BlockSpec(memory_space=pltpu.VMEM)
    return pl.pallas_call(
        spread_kernel,
        out_shape=jax.ShapeDtypeStruct((16, 128, 128), jnp.bfloat16),
        in_specs=[smem, smem, smem, vmem, vmem, vmem],
        out_specs=vmem,
        scratch_shapes=[
            pltpu.VMEM((17, 128, 128), jnp.float32),
        ],
        compiler_params=pltpu.CompilerParams(vmem_limit_bytes=20 * 2**20),
        name="spread_rows",
    )(rows, cols, count, sources, embeddings.reshape(16, 128, 128), adjacency)


CHUNKS = 4
ROWS = 512 // CHUNKS


def attend(flat, wide):
    across = lax.dot_general(
        wide, flat, (((1,), (1,)), ((), ())), preferred_element_type=jnp.float32
    )
    query = across[0:128] * (math.log2(math.e) / math.sqrt(HEAD))

    def heads(rows, b):
        return rows[:, b * ROWS : (b + 1) * ROWS].reshape(4, HEAD, ROWS)

    key = [heads(across[128:256], b) for b in range(4)]
    value = [heads(across[256:384], b) for b in range(4)]
    mixed = []
    for q in range(4):
        mine = heads(query, q)
        scores = [jnp.sum(mine * one, axis=1, keepdims=True) for one in key]
        top = jnp.maximum(jnp.maximum(scores[0], scores[1]), jnp.maximum(scores[2], scores[3]))
        weights = [jnp.exp2(one - top) for one in scores]
        share = 1.0 / ((weights[0] + weights[1]) + (weights[2] + weights[3]))
        blend = (weights[0] * share) * value[0]
        for b in range(1, 4):
            blend = blend + (weights[b] * share) * value[b]
        mixed.append(blend.reshape(128, ROWS).T.astype(jnp.bfloat16))
    return jnp.concatenate(mixed, axis=0)


def merge_kernel(
    spread_ref,
    wq_ref,
    wk_ref,
    wv_ref,
    wo_ref,
    gain_ref,
    up_ref,
    down_ref,
    out_ref,
    got,
    done,
    wide,
    own_sem,
    in_send,
    in_recv,
    out_send,
    out_recv,
):
    x, y, z, k = place()
    own = pltpu.make_async_copy(spread_ref.at[y], got.at[y], own_sem)
    own.start()
    barrier = pltpu.get_barrier_semaphore()
    for i in range(1, 4):
        pl.semaphore_signal(
            barrier, inc=1, device_id=device(x, lax.rem(y + i, 4), z, k), device_id_type=MESH
        )
    pl.semaphore_wait(barrier, 3)

    @pl.loop(0, CHUNKS)
    def _(c):
        span = pl.ds(pl.multiple_of(c * ROWS, ROWS), ROWS)
        for i in (2, 1, 3):
            there = lax.rem(y + i, 4)
            pltpu.make_async_remote_copy(
                src_ref=spread_ref.at[there, span],
                dst_ref=got.at[y, span],
                send_sem=in_send,
                recv_sem=in_recv.at[c],
                device_id=device(x, there, z, k),
                device_id_type=MESH,
            ).start()

    for i, ref in enumerate((wq_ref, wk_ref, wv_ref)):
        wide[i * 128 : (i + 1) * 128] = ref[...].astype(jnp.float32).T.astype(jnp.bfloat16)
    own.wait()

    @pl.loop(0, CHUNKS)
    def _(c):
        span = pl.ds(pl.multiple_of(c * ROWS, ROWS), ROWS)
        arrived = got.at[pl.ds(0, 3), span]
        pltpu.make_async_copy(arrived, arrived, in_recv.at[c]).wait()
        flat = got[:, span, :].reshape(4 * ROWS, 128)
        mixture = attend(flat, wide[...])
        residual = flat.astype(jnp.float32) + jnp.dot(
            mixture, wo_ref[...], preferred_element_type=jnp.float32
        )
        meansq = jnp.mean(residual * residual, axis=-1, keepdims=True)
        normed = (residual * lax.rsqrt(meansq + 1e-06) * gain_ref[...]).astype(jnp.bfloat16)
        hidden = jax.nn.silu(
            jnp.dot(normed, up_ref[...], preferred_element_type=jnp.float32)
        ).astype(jnp.bfloat16)
        result = residual + jnp.dot(hidden, down_ref[...], preferred_element_type=jnp.float32)
        done[:, span, :] = result.astype(jnp.bfloat16).reshape(4, ROWS, 128)
        for i in (2, 1, 3):
            there = lax.rem(y + i, 4)
            pltpu.make_async_remote_copy(
                src_ref=done.at[there, span],
                dst_ref=out_ref.at[y, span],
                send_sem=out_send,
                recv_sem=out_recv,
                device_id=device(x, there, z, k),
                device_id_type=MESH,
            ).start()

    own = pltpu.make_async_copy(done.at[y], out_ref.at[y], own_sem)
    own.start()
    own.wait()
    three = got.at[pl.ds(0, 3)]
    pltpu.make_async_copy(three, three, in_send).wait()
    pltpu.make_async_copy(three, three, out_send).wait()
    pltpu.make_async_copy(three, three, out_recv).wait()


def merge_rows(spread, w_query, w_key, w_value, w_out, mlp_gain, w_up, w_down):
    dma = pltpu.SemaphoreType.DMA
    vmem = pl.BlockSpec(memory_space=pltpu.VMEM)
    quarters = (4, 512, 128)
    return pl.pallas_call(
        merge_kernel,
        out_shape=jax.ShapeDtypeStruct(quarters, jnp.bfloat16),
        in_specs=[vmem] * 8,
        out_specs=vmem,
        scratch_shapes=[
            pltpu.VMEM(quarters, jnp.bfloat16),
            pltpu.VMEM(quarters, jnp.bfloat16),
            pltpu.VMEM((384, 128), jnp.bfloat16),
            dma,
            dma,
            dma((CHUNKS,)),
            dma,
            dma,
        ],
        compiler_params=pltpu.CompilerParams(
            collective_id=1, has_side_effects=True, vmem_limit_bytes=24 * 2**20
        ),
        name="merge_rows",
    )(
        spread.reshape(quarters),
        w_query,
        w_key,
        w_value,
        w_out,
        mlp_gain.reshape(1, 128),
        w_up,
        w_down,
    )


def shards(
    embeddings,
    adjacency,
    tile_rows,
    tile_cols,
    tile_count,
    need_ids,
    w_query,
    w_key,
    w_value,
    w_out,
    mlp_gain,
    w_up,
    w_down,
):
    sources = gather_sources(embeddings, need_ids)
    spread = spread_rows(tile_rows, tile_cols, tile_count, sources, embeddings, adjacency[0])
    merged = merge_rows(spread, w_query, w_key, w_value, w_out, mlp_gain, w_up, w_down)
    return merged.reshape(1, *embeddings.shape)


def solution(mesh):
    in_specs = (
        P("node", None),
        P("beh", "node", None, None),
        P("beh", "node"),
        P("beh", "node"),
        P("beh", "node"),
        P("beh", "node"),
        P(),
        P(),
        P(),
        P(),
        P(),
        P(),
        P(),
    )
    out_specs = P("beh", "node", None)
    return jax.shard_map(shards, mesh=mesh, in_specs=in_specs, out_specs=out_specs, check_vma=False)
```

```python
import functools
import math

import jax
import jax.numpy as jnp
from jax import lax
from jax.experimental import pallas as pl
from jax.experimental.pallas import tpu as pltpu
from jax.sharding import PartitionSpec as P

HEAD = 32
MESH = pl.DeviceIdType.MESH
STEPS = 8
FAR_FIRST = sorted(
    ((i, j) for i in range(4) for j in range(8) if i or j),
    key=lambda at: (-(min(at[0], 4 - at[0]) * 2 + min(at[1], 8 - at[1])) , (at[0] + at[1]) % 2),
)


def place():
    y = lax.axis_index("beh")
    n = lax.axis_index("node")
    return n // 32, y, lax.rem(n // 2, 16), lax.rem(n, 2)


def device(x, y, z, k):
    return (y, (x * 16 + z) * 2 + k)


def gather_kernel(emb_ref, need_ref, out_ref, *scratch):
    chunks = scratch[:9]
    picked, need_x, need_v, need_s = scratch[9:13]
    own_sem, pair_send, pair_recv, ring_send, ring_recv = scratch[13:18]
    ask_send, ask_recv, smem_sem, need_sem, y_send, y_recv = scratch[18:]
    x, y, z, k = place()
    part = y * 2 + k
    above = device(x, y, lax.rem(z + 1, 16), k)
    below = device(x, y, lax.rem(z + 15, 16), k)
    twin = device(x, y, z, 1 - k)
    rows = [lax.rem(x + i, 4) for i in range(4)]
    parts = [lax.rem(part + i, 8) for i in range(8)]
    row_peers = [device(xx, y, z, k) for xx in rows]
    part_peers = [device(x, p // 2, z, lax.rem(p, 2)) for p in parts]

    def send(src, dst, sent, landed, where):
        copy = pltpu.make_async_remote_copy(
            src_ref=src,
            dst_ref=dst,
            send_sem=sent,
            recv_sem=landed,
            device_id=where,
            device_id_type=MESH,
        )
        copy.start()
        return copy

    def wait_bytes(ref, sem):
        pltpu.make_async_copy(ref, ref, sem).wait()

    own = pltpu.make_async_copy(
        emb_ref.at[:, part], chunks[0].at[pl.ds(k * 16, 16)], own_sem
    )
    own.start()
    mine = pltpu.make_async_copy(need_ref, need_x.at[x], need_sem)
    mine.start()

    barrier = pltpu.get_barrier_semaphore()
    for peer in (above, below, *row_peers[1:], *part_peers[1:]):
        pl.semaphore_signal(barrier, inc=1, device_id=peer, device_id_type=MESH)
    pl.semaphore_wait(barrier, 12)

    def half(step, way, h):
        core = k if h < 2 else 1 - k
        blocks = pl.ds(core * 16 + (h % 2) * 8, 8)
        if step == 0 or step == STEPS:
            return chunks[step].at[blocks]
        return chunks[step].at[way, blocks]

    hops = {}

    def forward(step, h):
        for way in range(2):
            if (step - 1, way, h) in hops:
                hops[(step - 1, way, h)].wait_recv()
            if step < STEPS - 1 or (step < STEPS and way == h % 2):
                hops[(step, way, h)] = send(
                    half(step, way, h),
                    half(step + 1, way, h),
                    ring_send.at[way, step, h],
                    ring_recv.at[way, step, h],
                    above if way == 0 else below,
                )

    def third(step):
        return 0 if step == 0 else 2 if step == STEPS else 1

    def pick(step, low=0, high=8):
        @pl.loop(low, high)
        def _(p):
            for xx in range(4):
                if step == 0:
                    index = lax.rem(need_s[p, xx, 0, x * 16 + z], 32)
                    picked[0, xx * 8 + p, 0] = chunks[0][index]
                elif step == STEPS:
                    index = lax.rem(need_s[p, xx, 0, x * 16 + lax.rem(z + 8, 16)], 32)
                    picked[STEPS, xx * 8 + p, 0] = chunks[STEPS][index]
                else:
                    index = lax.rem(need_s[p, xx, 0, x * 16 + lax.rem(z + 16 - step, 16)], 32)
                    picked[step, xx * 8 + p, 0] = chunks[step][0, index]
                    index = lax.rem(need_s[p, xx, 0, x * 16 + lax.rem(z + step, 16)], 32)
                    picked[step, xx * 8 + p, 1] = chunks[step][1, index]

    me = x * 8 + part

    def deliver(step):
        width = pl.ds(0, 1 if step == 0 or step == STEPS else 2)
        turn = third(step)
        pltpu.make_async_copy(
            picked.at[step, me, width], out_ref.at[step, part, x, width], y_recv.at[turn]
        ).start()
        for i, j in FAR_FIRST:
            send(
                picked.at[step, rows[i] * 8 + parts[j], width],
                out_ref.at[step, part, x, width],
                y_send.at[turn],
                y_recv.at[turn],
                device(rows[i], parts[j] // 2, z, lax.rem(parts[j], 2)),
            )

    mine.wait()
    for i in (2, 1, 3):
        send(need_x.at[x], need_x.at[x], ask_send.at[0], ask_recv.at[0], row_peers[i])
    pair = send(
        emb_ref.at[:, y * 2 + 1 - k],
        chunks[0].at[pl.ds(k * 16, 16)],
        pair_send,
        pair_recv,
        twin,
    )
    own.wait()
    forward(0, 0)
    forward(0, 1)
    wait_bytes(need_x.at[pl.ds(0, 3)], ask_recv.at[0])
    for i in (4, 5, 3, 2, 6, 7, 1):
        send(need_x, need_s.at[part], ask_send.at[1], ask_recv.at[1], part_peers[i])
    pltpu.make_async_copy(need_x, need_s.at[part], ask_recv.at[1]).start()
    pair.wait_recv()
    forward(0, 2)
    forward(0, 3)
    forward(1, 0)
    forward(1, 1)
    wait_bytes(need_s, ask_recv.at[1])
    forward(1, 2)
    forward(1, 3)
    pick(0)
    deliver(0)
    pick(1)
    deliver(1)
    for step in range(2, STEPS + 1):
        for h in range(4):
            forward(step, h)
        pick(step)
        deliver(step)

    pair.wait_send()
    for one in hops.values():
        one.wait_send()
    wait_bytes(need_x.at[pl.ds(0, 3)], ask_send.at[0])
    wait_bytes(need_v.at[pl.ds(0, 7)], ask_send.at[1])
    ends = ((0, pl.ds(0, 1), pl.ds(0, 1)), (1, pl.ds(1, 7), pl.ds(0, 2)), (2, pl.ds(8, 1), pl.ds(0, 1)))
    for turn, steps, width in ends:
        wait_bytes(picked.at[steps, pl.ds(0, 31), width], y_send.at[turn])
        wait_bytes(out_ref.at[steps, :, :, width], y_recv.at[turn])


def gather_sources(embeddings, need):
    dma = pltpu.SemaphoreType.DMA
    one = pltpu.VMEM((32, 16, 128), jnp.bfloat16)
    two = pltpu.VMEM((2, 32, 16, 128), jnp.bfloat16)
    picks = pltpu.VMEM((9, 32, 2, 16, 128), jnp.bfloat16)
    return pl.pallas_call(
        gather_kernel,
        out_shape=jax.ShapeDtypeStruct((9, 8, 4, 2, 16, 128), jnp.bfloat16),
        in_specs=[pl.BlockSpec(memory_space=pltpu.HBM)] * 2,
        out_specs=pl.BlockSpec(memory_space=pltpu.VMEM),
        scratch_shapes=[
            one,
            *([two] * 7),
            one,
            picks,
            pltpu.VMEM((4, 1, 64), jnp.int32),
            pltpu.VMEM((8, 4, 1, 64), jnp.int32),
            pltpu.SMEM((8, 4, 1, 64), jnp.int32),
            dma,
            dma,
            dma,
            dma((2, 8, 4)),
            dma((2, 8, 4)),
            dma((2,)),
            dma((2,)),
            dma,
            dma,
            dma((3,)),
            dma((3,)),
        ],
        compiler_params=pltpu.CompilerParams(
            collective_id=0, has_side_effects=True, vmem_limit_bytes=16 * 2**20
        ),
        cost_estimate=pl.CostEstimate(
            flops=2**33, transcendentals=0, bytes_accessed=2**26
        ),
        name="gather_sources",
    )(
        pltpu.with_memory_space_constraint(embeddings.reshape(16, 8, 16, 128), pltpu.HBM),
        pltpu.with_memory_space_constraint(need, pltpu.HBM),
    )


GROUP = 16
TILES = 112


def spread_kernel(rows_ref, cols_ref, count_ref, src_ref, emb_ref, adj_ref, out_ref, acc):
    z = place()[2]
    count = count_ref[0, 0]

    acc[0:16] = emb_ref[...].astype(jnp.float32)

    def add(t):
        col = cols_ref[0, t]
        away = lax.rem(lax.rem(col, 16) - z + 16, 16)
        step = jnp.minimum(away, 16 - away)
        way = jnp.where((away > 0) & (away < 8), 1, 0)
        row = jnp.where(t < count, rows_ref[0, t], 16)
        product = jnp.dot(
            adj_ref[t], src_ref[step, :, col // 16, way].reshape(128, 128), preferred_element_type=jnp.float32
        )
        acc[row] += product

    @pl.loop(0, (count + GROUP - 1) // GROUP)
    def _(i):
        for j in range(GROUP):
            add(i * GROUP + j)

    out_ref[...] = acc[0:16].astype(jnp.bfloat16)


def spread_rows(rows, cols, count, sources, embeddings, adjacency):
    smem = pl.BlockSpec(memory_space=pltpu.SMEM)
    vmem = pl.BlockSpec(memory_space=pltpu.VMEM)
    return pl.pallas_call(
        spread_kernel,
        out_shape=jax.ShapeDtypeStruct((16, 128, 128), jnp.bfloat16),
        in_specs=[smem, smem, smem, vmem, vmem, vmem],
        out_specs=vmem,
        scratch_shapes=[
            pltpu.VMEM((17, 128, 128), jnp.float32),
        ],
        compiler_params=pltpu.CompilerParams(vmem_limit_bytes=20 * 2**20),
        name="spread_rows",
    )(rows, cols, count, sources, embeddings.reshape(16, 128, 128), adjacency)


CHUNKS = 4
ROWS = 512 // CHUNKS


def attend(flat, wide):
    across = lax.dot_general(
        wide, flat, (((1,), (1,)), ((), ())), preferred_element_type=jnp.float32
    )
    query = across[0:128] * (math.log2(math.e) / math.sqrt(HEAD))

    def heads(rows, b):
        return rows[:, b * ROWS : (b + 1) * ROWS].reshape(4, HEAD, ROWS)

    key = [heads(across[128:256], b) for b in range(4)]
    value = [heads(across[256:384], b) for b in range(4)]
    mixed = []
    for q in range(4):
        mine = heads(query, q)
        scores = [jnp.sum(mine * one, axis=1, keepdims=True) for one in key]
        top = jnp.maximum(jnp.maximum(scores[0], scores[1]), jnp.maximum(scores[2], scores[3]))
        weights = [jnp.exp2(one - top) for one in scores]
        share = 1.0 / ((weights[0] + weights[1]) + (weights[2] + weights[3]))
        blend = (weights[0] * share) * value[0]
        for b in range(1, 4):
            blend = blend + (weights[b] * share) * value[b]
        mixed.append(blend.reshape(128, ROWS).T.astype(jnp.bfloat16))
    return jnp.concatenate(mixed, axis=0)


def merge_kernel(
    spread_ref,
    wq_ref,
    wk_ref,
    wv_ref,
    wo_ref,
    gain_ref,
    up_ref,
    down_ref,
    out_ref,
    got,
    done,
    wide,
    own_sem,
    in_send,
    in_recv,
    out_send,
    out_recv,
):
    x, y, z, k = place()
    own = pltpu.make_async_copy(spread_ref.at[y], got.at[y], own_sem)
    own.start()
    barrier = pltpu.get_barrier_semaphore()
    for i in range(1, 4):
        pl.semaphore_signal(
            barrier, inc=1, device_id=device(x, lax.rem(y + i, 4), z, k), device_id_type=MESH
        )
    pl.semaphore_wait(barrier, 3)

    @pl.loop(0, CHUNKS)
    def _(c):
        span = pl.ds(pl.multiple_of(c * ROWS, ROWS), ROWS)
        for i in (2, 1, 3):
            there = lax.rem(y + i, 4)
            pltpu.make_async_remote_copy(
                src_ref=spread_ref.at[there, span],
                dst_ref=got.at[y, span],
                send_sem=in_send,
                recv_sem=in_recv.at[c],
                device_id=device(x, there, z, k),
                device_id_type=MESH,
            ).start()

    for i, ref in enumerate((wq_ref, wk_ref, wv_ref)):
        wide[i * 128 : (i + 1) * 128] = ref[...].astype(jnp.float32).T.astype(jnp.bfloat16)
    own.wait()

    @pl.loop(0, CHUNKS)
    def _(c):
        span = pl.ds(pl.multiple_of(c * ROWS, ROWS), ROWS)
        arrived = got.at[pl.ds(0, 3), span]
        pltpu.make_async_copy(arrived, arrived, in_recv.at[c]).wait()
        flat = got[:, span, :].reshape(4 * ROWS, 128)
        mixture = attend(flat, wide[...])
        residual = flat.astype(jnp.float32) + jnp.dot(
            mixture, wo_ref[...], preferred_element_type=jnp.float32
        )
        meansq = jnp.mean(residual * residual, axis=-1, keepdims=True)
        normed = (residual * lax.rsqrt(meansq + 1e-06) * gain_ref[...]).astype(jnp.bfloat16)
        hidden = jax.nn.silu(
            jnp.dot(normed, up_ref[...], preferred_element_type=jnp.float32)
        ).astype(jnp.bfloat16)
        result = residual + jnp.dot(hidden, down_ref[...], preferred_element_type=jnp.float32)
        done[:, span, :] = result.astype(jnp.bfloat16).reshape(4, ROWS, 128)
        for i in (2, 1, 3):
            there = lax.rem(y + i, 4)
            pltpu.make_async_remote_copy(
                src_ref=done.at[there, span],
                dst_ref=out_ref.at[y, span],
                send_sem=out_send,
                recv_sem=out_recv,
                device_id=device(x, there, z, k),
                device_id_type=MESH,
            ).start()

    own = pltpu.make_async_copy(done.at[y], out_ref.at[y], own_sem)
    own.start()
    own.wait()
    three = got.at[pl.ds(0, 3)]
    pltpu.make_async_copy(three, three, in_send).wait()
    pltpu.make_async_copy(three, three, out_send).wait()
    pltpu.make_async_copy(three, three, out_recv).wait()


def merge_rows(spread, w_query, w_key, w_value, w_out, mlp_gain, w_up, w_down):
    dma = pltpu.SemaphoreType.DMA
    vmem = pl.BlockSpec(memory_space=pltpu.VMEM)
    quarters = (4, 512, 128)
    return pl.pallas_call(
        merge_kernel,
        out_shape=jax.ShapeDtypeStruct(quarters, jnp.bfloat16),
        in_specs=[vmem] * 8,
        out_specs=vmem,
        scratch_shapes=[
            pltpu.VMEM(quarters, jnp.bfloat16),
            pltpu.VMEM(quarters, jnp.bfloat16),
            pltpu.VMEM((384, 128), jnp.bfloat16),
            dma,
            dma,
            dma((CHUNKS,)),
            dma,
            dma,
        ],
        compiler_params=pltpu.CompilerParams(
            collective_id=1, has_side_effects=True, vmem_limit_bytes=24 * 2**20
        ),
        name="merge_rows",
    )(
        spread.reshape(quarters),
        w_query,
        w_key,
        w_value,
        w_out,
        mlp_gain.reshape(1, 128),
        w_up,
        w_down,
    )


def shards(
    embeddings,
    adjacency,
    tile_rows,
    tile_cols,
    tile_count,
    need_ids,
    w_query,
    w_key,
    w_value,
    w_out,
    mlp_gain,
    w_up,
    w_down,
):
    sources = gather_sources(embeddings, need_ids)
    spread = spread_rows(tile_rows, tile_cols, tile_count, sources, embeddings, adjacency[0])
    merged = merge_rows(spread, w_query, w_key, w_value, w_out, mlp_gain, w_up, w_down)
    return merged.reshape(1, *embeddings.shape)


def solution(mesh):
    in_specs = (
        P("node", None),
        P("beh", "node", None, None),
        P("beh", "node"),
        P("beh", "node"),
        P("beh", "node"),
        P("beh", "node"),
        P(),
        P(),
        P(),
        P(),
        P(),
        P(),
        P(),
    )
    out_specs = P("beh", "node", None)
    return jax.shard_map(shards, mesh=mesh, in_specs=in_specs, out_specs=out_specs, check_vma=False)
```
